32 devices in a mesh: conv: 2 (over x), seq: 8 (over z, y), head: 2 (over core).
Axes of the slice: x: 2, y: 2, z: 4, core: 2. Of those that a mesh axis runs over, the one named last changes fastest.
Arguments:
- queries: bfloat16 [3072, 2048], P(('conv', 'seq'), 'head'), parts along dimension 0, may hold values from -10 to 10, as said below
- key_states: bfloat16 [3072, 512], P(('conv', 'seq'), 'head'), parts along dimension 0, may hold values from -5 to 5, as said below
- value_states: bfloat16 [3072, 512], P(('conv', 'seq'), 'head'), parts along dimension 0, may hold values from -16 to 16
- out_weight: bfloat16 [2048, 4096], P('head'), may hold values from -0.125 to 0.125
- turn_lengths: int32 [32], P('conv'), parts along dimension 0, may hold values from 1 to 959, as said below
- block_flags: int32 [16, 8], P(('conv', 'seq')), parts along dimension 0, may hold values 0 or 1
Outputs:
- pooled: float32 [32, 4096], P(('conv', 'seq'), 'head'), parts along dimension 0
The draws below stay inside these ranges and needn't reach their ends.
There are 2 independent parts, one for each index of `conv`. The reference program is written for one: setup_inputs(seed, part) draws one part's arguments, and reference() takes and returns one part's arrays. A program takes and returns all parts, laid end to end along the dimension named above; an argument that names none is the same for every part. Nothing has to cross between parts.
Inputs may be any that keep to these rules, and one draw needn't show every extreme that they name: `queries`: every entry lies within the stated bounds. `key_states`: every entry lies within the stated bounds. `turn_lengths`: the lengths sum to 1536; turn 0 has one token and turn 1, the longest, has exactly 959 tokens.
All inputs are finite; a program needn't handle non-finite values. No bound on the sum of `block_flags` on one device may be relied on, other than what follows from the above.
Results may differ from the reference program's by a relative error of at most 0.0035.
Values may be sent and summed in bfloat16 or wider, within the bound.
A program may use at most 128 MiB of HBM per device.

```python
import math
import jax
import jax.numpy as jnp
from jax import lax

D = 4096
HEADS = 16
KV_HEADS = 4
HD = 128
TOK_DEV = 192
TURN_DEV = 2
TOKENS = 1536
TURNS = 16
TURN_MOST = 959
NBLK = 8


def draw_queries(key, part):
    values_drawn = 2.5 * jax.random.normal(jax.random.fold_in(key, 1), (TOKENS, HEADS * HD), jnp.float32)
    return jnp.clip(values_drawn, -10.0, 10.0).astype(jnp.bfloat16)


def draw_key_states(key, part):
    values_drawn = jax.random.normal(jax.random.fold_in(key, 2), (TOKENS, KV_HEADS * HD), jnp.float32)
    return jnp.clip(values_drawn, -5.0, 5.0).astype(jnp.bfloat16)


def draw_turn_lengths(key, part):
    remain_tokens = TOKENS - TURN_MOST - (TURN_DEV - 1)
    remain_turns = TURNS - TURN_DEV
    picked = jax.random.permutation(jax.random.fold_in(key, 21), remain_tokens - 1)[:remain_turns - 1] + 1
    cuts = jnp.sort(picked.astype(jnp.int32))
    bounds = jnp.concatenate([jnp.zeros((1,), jnp.int32), cuts, jnp.full((1,), remain_tokens, jnp.int32)])
    rest = (bounds[1:] - bounds[:-1]).astype(jnp.int32)
    leading = jnp.concatenate([jnp.ones((TURN_DEV - 1,), jnp.int32), jnp.full((1,), TURN_MOST, jnp.int32)])
    return jnp.concatenate([leading, rest]).astype(jnp.int32)


def set_ends(values, own_key, smallest, largest):
    extent = values.shape
    spot = [jax.random.randint(jax.random.fold_in(own_key, axis), (), 0, extent[axis]) for axis in range(len(extent))]
    values = values.at[tuple(spot)].set(smallest)
    longest = extent.index(max(extent))
    spot[longest] = (spot[longest] + 1) % extent[longest]
    return values.at[tuple(spot)].set(largest)


def level_of(stream_key, shape, shards, least, largest):
    def one(position, parts):
        heights = jax.random.uniform(jax.random.fold_in(jax.random.fold_in(stream_key, 6), position), (parts,), jnp.float32, least / len(shards), largest / len(shards))
        return jnp.repeat(jnp.exp(heights), shape[position] // parts).reshape((-1,) + (1,) * (len(shape) - position - 1))

    gain = one(*shards[0])
    for cut in shards[1:]:
        gain = gain * one(*cut)
    return gain


def normal_values(own_key, shape, scale, reach, cuts=(), held_as=jnp.bfloat16):
    values = scale * jax.random.normal(own_key, shape, jnp.float32)
    if cuts:
        values = values * level_of(own_key, shape, cuts, -0.22, 0.18)
    return jnp.clip(values, -reach, reach).astype(held_as)


def setup_inputs(seed: int = 0, part: int = 0) -> dict:
    streams_of = jax.random.split(jax.random.key(seed), 7)
    part_keys = jax.random.split(jax.random.fold_in(streams_of[6], part), 7)
    queries = draw_queries(jax.random.fold_in(jax.random.fold_in(streams_of[6], part), 71), part)
    key_states = draw_key_states(jax.random.fold_in(jax.random.fold_in(streams_of[6], part), 71), part)
    value_states = normal_values(part_keys[2], (TOKENS, KV_HEADS * HD), 4.0, 16.0, ((0, 8), (1, 2)))
    out_weight = normal_values(streams_of[3], (HEADS * HD, D), (HEADS * HD) ** -0.5, 0.125, ((0, 2),))
    turn_lengths = draw_turn_lengths(jax.random.fold_in(jax.random.fold_in(streams_of[6], part), 71), part)
    block_flags = set_ends((jax.random.randint(part_keys[5], (NBLK, NBLK), 0, 4) < 3).astype(jnp.int32), jax.random.fold_in(part_keys[5], 1), 0, 1)
    return dict(queries=queries, key_states=key_states, value_states=value_states, out_weight=out_weight, turn_lengths=turn_lengths, block_flags=block_flags)


big_negative = -1e+30
log_two_e = 1.4426950408889634

def reference(queries, key_states, value_states, out_weight, turn_lengths, block_flags):
    repeat = HEADS // KV_HEADS
    factor = log_two_e / math.sqrt(HD)
    key_all = key_states.reshape(TOKENS, KV_HEADS, HD).astype(jnp.float32)
    value_all = value_states.reshape(TOKENS, KV_HEADS, HD).astype(jnp.float32)
    key_pos = jnp.arange(TOKENS, dtype=jnp.int32)
    key_block = key_pos // TOK_DEV
    q_block = math.gcd(TOKENS, 512)
    block_total = TOKENS // q_block

    def one_block(number):
        start = (number * q_block).astype(jnp.int32)
        query_rows = lax.dynamic_slice_in_dim(queries, start, q_block, 0)
        query_rows = query_rows.reshape(q_block, KV_HEADS, repeat, HD).astype(jnp.float32)
        query_pos = start + jnp.arange(q_block, dtype=jnp.int32)
        query_block = query_pos // TOK_DEV
        flag_table = block_flags[query_block][:, key_block]
        visible = (key_pos[None, :] <= query_pos[:, None]) & ((key_block[None, :] == query_block[:, None]) | (flag_table == 1))
        logit = jnp.einsum('qgrd,kgd->grqk', query_rows, key_all) * factor
        logit = jnp.where(visible[None, None], logit, big_negative)
        row_top = jnp.ceil(lax.optimization_barrier(jnp.max(logit, axis=-1)))
        weights = jnp.where(visible[None, None], jnp.exp2(logit - row_top[..., None]), 0.0)
        weight_sum = lax.optimization_barrier(jnp.sum(weights, axis=-1))
        rounded = lax.optimization_barrier(weights.astype(jnp.bfloat16)).astype(jnp.float32)
        output = jnp.einsum('grqk,kgd->grqd', rounded, value_all) / weight_sum[..., None]
        return output.transpose(2, 0, 1, 3).reshape(q_block, HEADS * HD).astype(jnp.bfloat16)
    blocks = lax.map(one_block, jnp.arange(block_total, dtype=jnp.int32))
    attended = blocks.reshape(TOKENS, HEADS * HD)
    projected = jnp.dot(attended, out_weight, preferred_element_type=jnp.float32)
    turn_ends = jnp.cumsum(turn_lengths).astype(jnp.int32)
    starts = turn_ends - turn_lengths
    member = (starts[:, None] <= key_pos[None, :]) & (key_pos[None, :] < turn_ends[:, None])
    turn_share = jnp.where(member, 1.0, 0.0).astype(jnp.float32) / turn_lengths[:, None].astype(jnp.float32)
    return jnp.dot(turn_share, projected, precision=lax.Precision.HIGHEST)
```

```python
import functools
import math

import jax
import jax.numpy as jnp
from jax import lax
from jax.experimental import pallas as pl
from jax.experimental.pallas import tpu as pltpu
from jax.sharding import PartitionSpec as P

HD = 128
CHUNK = 256
MESH = pl.DeviceIdType.MESH
big_negative = -1e30
log_two_e = 1.4426950408889634


def kernel(
    dims,
    q_hbm,
    k_hbm,
    v_hbm,
    w_hbm,
    len_ref,
    flag_ref,
    out_ref,
    kv,
    q_in,
    q_rows,
    q_turned,
    weight,
    top,
    total,
    acc,
    member,
    part,
    parts,
    lhs,
    half_out,
    half_in,
    local_sem,
    weight_sem,
    line_send,
    row_send,
    recv,
    part_send,
    part_recv,
    half_send,
    half_recv,
):
    n, inner, rows, heads, groups, turns, owned = dims
    outer = n // inner
    repeat = heads // groups
    wide = heads * rows
    factor = log_two_e / math.sqrt(HD)
    me = lax.axis_index("seq")
    head = lax.axis_index("head")
    o, i = lax.div(me, inner), lax.rem(me, inner)

    barrier = pltpu.get_barrier_semaphore()
    for j in range(1, n):
        pl.semaphore_signal(
            barrier, inc=1, device_id={"seq": lax.rem(me + j, n)}, device_id_type=MESH
        )
    pl.semaphore_signal(barrier, inc=1, device_id={"head": 1 - head}, device_id_type=MESH)

    cols = weight.shape[2]
    loads = [
        pltpu.make_async_copy(q_hbm, q_in, local_sem.at[0]),
        pltpu.make_async_copy(k_hbm, kv.at[me, 0], local_sem.at[1]),
        pltpu.make_async_copy(v_hbm, kv.at[me, 1], local_sem.at[2]),
    ]
    for load in loads:
        load.start()
    pl.semaphore_wait(barrier, n)

    def line_copy(kind, d, source):
        b = me - d * inner
        return pltpu.make_async_remote_copy(
            src_ref=source,
            dst_ref=kv.at[b, kind],
            send_sem=line_send.at[kind, d],
            recv_sem=recv.at[kind, b],
            device_id={"seq": lax.rem(me + inner, n)},
            device_id_type=MESH,
        )

    def row_copy(kind, d, j, source):
        b = me - d * inner
        return pltpu.make_async_remote_copy(
            src_ref=source,
            dst_ref=kv.at[b, kind],
            send_sem=row_send.at[kind, d, j],
            recv_sem=recv.at[kind, b],
            device_id={"seq": o * inner + lax.rem(i + j, inner)},
            device_id_type=MESH,
        )

    def sends(kind, d, source, act, own):
        @pl.when(o < outer - 1)
        def _():
            act(line_copy(kind, d, source))

        for j in range(1, inner):
            if own:

                @pl.when(lax.rem(i + j, inner) > i)
                def _():
                    act(row_copy(kind, d, j, source))

            else:
                act(row_copy(kind, d, j, source))

    def begin(copy):
        copy.start()

    def finish(copy):
        copy.wait_send()

    def arrived(kind, b):
        pltpu.make_async_copy(kv.at[b, kind], kv.at[b, kind], recv.at[kind, b]).wait()

    sends(0, 0, k_hbm, begin, True)
    sends(1, 0, v_hbm, begin, True)
    weight_loads = []
    for slot, side in ((0, 1 - head), (1, head)):
        start = pl.multiple_of(side * cols, cols)
        weight_loads.append(
            pltpu.make_async_copy(
                w_hbm.at[:, pl.ds(start, cols)], weight.at[slot], weight_sem.at[slot]
            )
        )
    for load in weight_loads:
        load.start()

    for load in loads:
        load.wait()
    for h in range(heads):
        q_rows[h * rows : (h + 1) * rows, :] = q_in[:, h * HD : (h + 1) * HD]
    q_turned[...] = q_rows[...].T

    def attend(b, diagonal):
        if not diagonal:
            seen = jnp.full((1, CHUNK), flag_ref[0, b], jnp.int32) == 1
        for g in range(groups):
            keys = kv[b, 0, :, g * HD : (g + 1) * HD]
            values = kv[b, 1, :, g * HD : (g + 1) * HD].T
            for c in range(g * repeat * rows, (g + 1) * repeat * rows, CHUNK):
                here = slice(c, c + CHUNK)
                logit = jnp.dot(keys, q_turned[:, here], preferred_element_type=jnp.float32)
                if diagonal:
                    column = c + lax.broadcasted_iota(jnp.int32, (1, CHUNK), 1)
                    token = column
                    for h in range(1, heads):
                        token = jnp.where(column >= h * rows, column - h * rows, token)
                    key = lax.broadcasted_iota(jnp.int32, (rows, CHUNK), 0)
                    logit = jnp.where(key <= token, logit, big_negative)
                    new_top = jnp.ceil(jnp.max(logit, axis=0, keepdims=True) * factor)
                    shift = new_top
                else:
                    old_top = top[:, here]
                    block_top = jnp.ceil(jnp.max(logit, axis=0, keepdims=True) * factor)
                    new_top = jnp.maximum(old_top, jnp.where(seen, block_top, big_negative))
                    shift = jnp.where(seen, new_top, -big_negative)
                weights = jnp.exp2(logit * factor - shift)
                added = jnp.sum(weights, axis=0, keepdims=True)
                update = jnp.dot(
                    values, weights.astype(jnp.bfloat16), preferred_element_type=jnp.float32
                )
                top[:, here] = new_top
                if diagonal:
                    total[:, here] = added
                    acc[:, here] = update
                else:
                    rescale = jnp.exp2(old_top - new_top)
                    total[:, here] = total[:, here] * rescale + added
                    acc[:, here] = acc[:, here] * rescale + update

    attend(me, True)

    lengths = len_ref[...].astype(jnp.float32)
    row = lax.broadcasted_iota(jnp.int32, (turns * heads, turns), 0)
    turn_of_row = lax.div(row, heads)
    head_of_row = (row - turn_of_row * heads)[:, :1].astype(jnp.float32)
    turn = lax.broadcasted_iota(jnp.int32, (turns * heads, turns), 1)
    spread = jnp.broadcast_to(lengths, (turns * heads, turns))
    starts = jnp.sum(jnp.where(turn < turn_of_row, spread, 0.0), axis=1, keepdims=True)
    length = jnp.sum(jnp.where(turn == turn_of_row, spread, 0.0), axis=1, keepdims=True)
    base = (me * rows).astype(jnp.float32)
    low = head_of_row * rows + jnp.clip(starts - base, 0.0, rows)
    high = head_of_row * rows + jnp.clip(starts + length - base, 0.0, rows)
    column = lax.broadcasted_iota(jnp.int32, (turns * heads, wide), 1).astype(jnp.float32)
    member[...] = jnp.where((column >= low) & (column < high), 1.0, 0.0).astype(jnp.bfloat16)
    share = 1.0 / length

    def row_blocks(d, own):
        for j in range(1, inner):
            place = lax.rem(i + j, inner)
            b = (o - d) * inner + place

            def take():
                arrived(0, b)
                arrived(1, b)
                attend(b, False)

            if own:
                pl.when(place < i)(take)
            else:
                take()

    row_blocks(0, True)

    def step(d, carry):
        b = me - d * inner
        arrived(0, b)
        sends(0, d, kv.at[b, 0], begin, False)
        arrived(1, b)
        sends(1, d, kv.at[b, 1], begin, False)
        attend(b, False)
        row_blocks(d, False)
        return carry

    lax.fori_loop(1, o + 1, step, 0)

    attended = (acc[...] * (1.0 / total[...])).astype(jnp.bfloat16)
    pooled = lax.dot_general(
        member[...],
        attended,
        (((1,), (1,)), ((), ())),
        preferred_element_type=jnp.float32,
    )
    part[...] = (pooled * share).reshape(turns, heads, HD)

    def part_copy(j):
        peer = lax.rem(me + j, n)
        return pltpu.make_async_remote_copy(
            src_ref=part.at[pl.ds(peer * owned, owned)],
            dst_ref=parts.at[me],
            send_sem=part_send.at[j],
            recv_sem=part_recv.at[me],
            device_id={"seq": peer},
            device_id_type=MESH,
        )

    for j in range(1, n):
        part_copy(j).start()
    mine = part[pl.ds(me * owned, owned)]

    def gather(j, summed):
        peer = lax.rem(me + j, n)
        pltpu.make_async_copy(parts.at[peer], parts.at[peer], part_recv.at[peer]).wait()
        return summed + parts[peer]

    summed = lax.fori_loop(1, n, gather, mine)
    flat = jnp.concatenate([summed[:, h, :] for h in range(heads)], axis=1)
    high_part = flat.astype(jnp.bfloat16).astype(jnp.float32)
    rest = flat - high_part
    middle_part = rest.astype(jnp.bfloat16).astype(jnp.float32)
    lhs[...] = jnp.zeros_like(lhs)
    lhs[0:owned, :] = high_part
    lhs[owned : 2 * owned, :] = middle_part
    lhs[2 * owned : 3 * owned, :] = rest - middle_part
    operand = lhs[...].astype(jnp.bfloat16)

    def project(slot):
        weight_loads[slot].wait()
        wide_out = jnp.dot(operand, weight[slot], preferred_element_type=jnp.float32)
        return (
            wide_out[0:owned] + wide_out[owned : 2 * owned] + wide_out[2 * owned : 3 * owned]
        )

    half_out[...] = project(0)
    half = pltpu.make_async_remote_copy(
        src_ref=half_out,
        dst_ref=half_in,
        send_sem=half_send,
        recv_sem=half_recv,
        device_id={"head": 1 - head},
        device_id_type=MESH,
    )
    half.start()
    own_half = project(1)

    sends(0, 0, k_hbm, finish, True)
    sends(1, 0, v_hbm, finish, True)

    def settle(d, carry):
        b = me - d * inner
        sends(0, d, kv.at[b, 0], finish, False)
        sends(1, d, kv.at[b, 1], finish, False)
        return carry

    lax.fori_loop(1, o + 1, settle, 0)
    for j in range(1, n):
        part_copy(j).wait_send()
    half.wait()
    out_ref[...] = own_half + half_in[...]


def on_device(n, nh, queries, key_states, value_states, out_weight, turn_lengths, block_flags):
    rows = queries.shape[0]
    heads = queries.shape[1] // HD
    groups = key_states.shape[1] // HD
    turns = turn_lengths.shape[0]
    owned = turns // n
    depth, width = out_weight.shape
    cols = width // nh
    inner = 2 if n <= 8 else 8
    outer = n // inner
    wide = heads * rows
    dims = (n, inner, rows, heads, groups, turns, owned)
    lhs_rows = -(-3 * owned // 8) * 8
    dma = pltpu.SemaphoreType.DMA
    any_spec = pl.BlockSpec(memory_space=pl.ANY)
    return pl.pallas_call(
        functools.partial(kernel, dims),
        out_shape=jax.ShapeDtypeStruct((owned, cols), jnp.float32),
        in_specs=[any_spec] * 4
        + [
            pl.BlockSpec(memory_space=pltpu.VMEM),
            pl.BlockSpec(memory_space=pltpu.SMEM),
        ],
        out_specs=pl.BlockSpec(memory_space=pltpu.VMEM),
        scratch_shapes=[
            pltpu.VMEM((n, 2, rows, groups * HD), jnp.bfloat16),
            pltpu.VMEM((rows, heads * HD), jnp.bfloat16),
            pltpu.VMEM((wide, HD), jnp.bfloat16),
            pltpu.VMEM((HD, wide), jnp.bfloat16),
            pltpu.VMEM((nh, depth, cols), jnp.bfloat16),
            pltpu.VMEM((1, wide), jnp.float32),
            pltpu.VMEM((1, wide), jnp.float32),
            pltpu.VMEM((HD, wide), jnp.float32),
            pltpu.VMEM((turns * heads, wide), jnp.bfloat16),
            pltpu.VMEM((turns, heads, HD), jnp.float32),
            pltpu.VMEM((n, owned, heads, HD), jnp.float32),
            pltpu.VMEM((lhs_rows, depth), jnp.float32),
            pltpu.VMEM((owned, cols), jnp.float32),
            pltpu.VMEM((owned, cols), jnp.float32),
            dma((3,)),
            dma((2,)),
            dma((2, outer)),
            dma((2, outer, inner)),
            dma((2, n)),
            dma((n,)),
            dma((n,)),
            dma,
            dma,
        ],
        compiler_params=pltpu.CompilerParams(
            collective_id=0, has_side_effects=True, vmem_limit_bytes=56 << 20
        ),
    )(
        queries,
        key_states,
        value_states,
        out_weight,
        turn_lengths.reshape(1, turns),
        block_flags,
    )


def solution(mesh):
    in_specs = (
        P(("conv", "seq"), "head"),
        P(("conv", "seq"), "head"),
        P(("conv", "seq"), "head"),
        P("head", None),
        P("conv"),
        P(("conv", "seq"), None),
    )
    out_specs = P(("conv", "seq"), "head")
    return jax.shard_map(
        functools.partial(on_device, mesh.shape["seq"], mesh.shape["head"]),
        mesh=mesh,
        in_specs=in_specs,
        out_specs=out_specs,
        check_vma=False,
    )
```

```python
import functools
import math

import jax
import jax.numpy as jnp
from jax import lax
from jax.experimental import pallas as pl
from jax.experimental.pallas import tpu as pltpu
from jax.sharding import PartitionSpec as P

HD = 128
CHUNK = 256
MESH = pl.DeviceIdType.MESH
big_negative = -1e30
log_two_e = 1.4426950408889634


def kernel(
    dims,
    q_hbm,
    k_hbm,
    v_hbm,
    w_hbm,
    len_ref,
    flag_ref,
    out_ref,
    kv,
    q_in,
    q_rows,
    q_turned,
    weight,
    top,
    total,
    acc,
    member,
    part,
    parts,
    lhs,
    local_sem,
    weight_sem,
    line_send,
    row_send,
    recv,
    side_send,
    part_send,
    part_recv,
):
    n, inner, rows, heads, groups, turns, owned = dims
    outer = n // inner
    repeat = heads // groups
    wide = heads * rows
    factor = log_two_e / math.sqrt(HD)
    me = lax.axis_index("seq")
    head = lax.axis_index("head")
    o, i = lax.div(me, inner), lax.rem(me, inner)

    barrier = pltpu.get_barrier_semaphore()
    for j in range(n):
        peer = lax.rem(me + j, n)
        for core in (1 - head, head) if j else (1 - head,):
            pl.semaphore_signal(
                barrier, inc=1, device_id={"seq": peer, "head": core}, device_id_type=MESH
            )

    cols = weight.shape[2]
    loads = [
        pltpu.make_async_copy(q_hbm, q_in, local_sem.at[0]),
        pltpu.make_async_copy(k_hbm, kv.at[me, 0], local_sem.at[1]),
        pltpu.make_async_copy(v_hbm, kv.at[me, 1], local_sem.at[2]),
    ]
    for load in loads:
        load.start()
    pl.semaphore_wait(barrier, 2 * n - 1)

    def line_copy(kind, d, source):
        b = me - d * inner
        return pltpu.make_async_remote_copy(
            src_ref=source,
            dst_ref=kv.at[b, kind],
            send_sem=line_send.at[kind, d],
            recv_sem=recv.at[kind, b],
            device_id={"seq": lax.rem(me + inner, n)},
            device_id_type=MESH,
        )

    def row_copy(kind, d, j, source):
        b = me - d * inner
        return pltpu.make_async_remote_copy(
            src_ref=source,
            dst_ref=kv.at[b, kind],
            send_sem=row_send.at[kind, d, j],
            recv_sem=recv.at[kind, b],
            device_id={"seq": o * inner + lax.rem(i + j, inner)},
            device_id_type=MESH,
        )

    def sends(kind, d, source, act, own):
        @pl.when(o < outer - 1)
        def _():
            act(line_copy(kind, d, source))

        for j in range(1, inner):
            if own:

                @pl.when(lax.rem(i + j, inner) > i)
                def _():
                    act(row_copy(kind, d, j, source))

            elif kind == 1 and inner == 2:

                @pl.when((i == 1) | (d > 1))
                def _():
                    act(row_copy(kind, d, j, source))

            else:
                act(row_copy(kind, d, j, source))

    def side_copy():
        b = o * inner
        return pltpu.make_async_remote_copy(
            src_ref=kv.at[b, 1],
            dst_ref=kv.at[b, 1],
            send_sem=side_send,
            recv_sem=recv.at[1, b],
            device_id={"seq": lax.rem(me + inner, n)},
            device_id_type=MESH,
        )

    def begin(copy):
        copy.start()

    def finish(copy):
        copy.wait_send()

    def arrived(kind, b):
        pltpu.make_async_copy(kv.at[b, kind], kv.at[b, kind], recv.at[kind, b]).wait()

    sends(0, 0, k_hbm, begin, True)
    sends(1, 0, v_hbm, begin, True)
    start = pl.multiple_of(head * cols, cols)
    other = pl.multiple_of((1 - head) * cols, cols)
    weight_load = pltpu.make_async_copy(
        w_hbm.at[:, pl.ds(start, cols)], weight.at[0], weight_sem.at[0]
    )
    weight_swap = pltpu.make_async_remote_copy(
        src_ref=w_hbm.at[:, pl.ds(other, cols)],
        dst_ref=weight.at[1],
        send_sem=weight_sem.at[1],
        recv_sem=weight_sem.at[2],
        device_id={"head": 1 - head},
        device_id_type=MESH,
    )
    weight_load.start()
    weight_swap.start()

    for load in loads:
        load.wait()
    for h in range(heads):
        q_rows[h * rows : (h + 1) * rows, :] = q_in[:, h * HD : (h + 1) * HD]
    q_turned[...] = q_rows[...].T

    def attend(b, diagonal):
        if not diagonal:
            seen = jnp.full((1, CHUNK), flag_ref[0, b], jnp.int32) == 1
        for g in range(groups):
            keys = kv[b, 0, :, g * HD : (g + 1) * HD]
            values = kv[b, 1, :, g * HD : (g + 1) * HD].T
            for c in range(g * repeat * rows, (g + 1) * repeat * rows, CHUNK):
                here = slice(c, c + CHUNK)
                logit = jnp.dot(keys, q_turned[:, here], preferred_element_type=jnp.float32)
                if diagonal:
                    column = c + lax.broadcasted_iota(jnp.int32, (1, CHUNK), 1)
                    token = column
                    for h in range(1, heads):
                        token = jnp.where(column >= h * rows, column - h * rows, token)
                    key = lax.broadcasted_iota(jnp.int32, (rows, CHUNK), 0)
                    logit = jnp.where(key <= token, logit, big_negative)
                    new_top = jnp.ceil(jnp.max(logit, axis=0, keepdims=True) * factor)
                    shift = new_top
                else:
                    old_top = top[:, here]
                    block_top = jnp.ceil(jnp.max(logit, axis=0, keepdims=True) * factor)
                    new_top = jnp.maximum(old_top, jnp.where(seen, block_top, big_negative))
                    shift = jnp.where(seen, new_top, -big_negative)
                weights = jnp.exp2(logit * factor - shift)
                added = jnp.sum(weights, axis=0, keepdims=True)
                update = jnp.dot(
                    values, weights.astype(jnp.bfloat16), preferred_element_type=jnp.float32
                )
                top[:, here] = new_top
                if diagonal:
                    total[:, here] = added
                    acc[:, here] = update
                else:
                    rescale = jnp.exp2(old_top - new_top)
                    total[:, here] = total[:, here] * rescale + added
                    acc[:, here] = acc[:, here] * rescale + update

    attend(me, True)

    lengths = len_ref[...].astype(jnp.float32)
    row = lax.broadcasted_iota(jnp.int32, (turns * heads, turns), 0)
    turn_of_row = lax.div(row, heads)
    head_of_row = (row - turn_of_row * heads)[:, :1].astype(jnp.float32)
    turn = lax.broadcasted_iota(jnp.int32, (turns * heads, turns), 1)
    spread = jnp.broadcast_to(lengths, (turns * heads, turns))
    starts = jnp.sum(jnp.where(turn < turn_of_row, spread, 0.0), axis=1, keepdims=True)
    length = jnp.sum(jnp.where(turn == turn_of_row, spread, 0.0), axis=1, keepdims=True)
    base = (me * rows).astype(jnp.float32)
    low = head_of_row * rows + jnp.clip(starts - base, 0.0, rows)
    high = head_of_row * rows + jnp.clip(starts + length - base, 0.0, rows)
    column = lax.broadcasted_iota(jnp.int32, (turns * heads, wide), 1).astype(jnp.float32)
    member[...] = jnp.where((column >= low) & (column < high), 1.0, 0.0).astype(jnp.bfloat16)
    share = 1.0 / length

    def row_blocks(d):
        for j in range(1, inner):
            place = lax.rem(i + j, inner)
            b = (o - d) * inner + place

            @pl.when((place < i) | (d > 0))
            def _():
                @pl.when((d > 0) | (inner != 2))
                def _():
                    arrived(0, b)
                    arrived(1, b)

                attend(b, False)

    if inner == 2:

        @pl.when(i == 1)
        def _():
            arrived(0, me - 1)
            arrived(1, me - 1)

            @pl.when(o < outer - 1)
            def _():
                side_copy().start()

    def step(d, carry):
        b = me - d * inner
        arrived(0, b)
        sends(0, d, kv.at[b, 0], begin, False)
        arrived(1, b)
        sends(1, d, kv.at[b, 1], begin, False)
        row_blocks(d - 1)
        attend(b, False)
        return carry

    lax.fori_loop(1, o + 1, step, 0)
    row_blocks(o)

    attended = (acc[...] * (1.0 / total[...])).astype(jnp.bfloat16)
    pooled = lax.dot_general(
        member[...],
        attended,
        (((1,), (1,)), ((), ())),
        preferred_element_type=jnp.float32,
    )
    part[...] = (pooled * share).reshape(turns, heads, HD)

    def part_copy(away, j):
        peer = lax.rem(me + j, n)
        return pltpu.make_async_remote_copy(
            src_ref=part.at[pl.ds(peer * owned, owned)],
            dst_ref=parts.at[head, me],
            send_sem=part_send.at[away, j],
            recv_sem=part_recv.at[head, me],
            device_id={"seq": peer, "head": 1 - head if away else head},
            device_id_type=MESH,
        )

    pairs = [(away, j) for j in range(n) for away in (0, 1) if away or j]
    for away, j in pairs:
        part_copy(away, j).start()

    def gather(away, j):
        peer = lax.rem(me + j, n)
        core = 1 - head if away else head
        here = parts.at[core, peer]
        pltpu.make_async_copy(here, here, part_recv.at[core, peer]).wait()
        return parts[core, peer]

    sums = [part[pl.ds(me * owned, owned)], None]
    for away, j in pairs:
        piece = gather(away, j)
        sums[away] = piece if sums[away] is None else sums[away] + piece

    lhs[...] = jnp.zeros_like(lhs)
    for slot, summed in enumerate(sums):
        flat = jnp.concatenate([summed[:, h, :] for h in range(heads)], axis=1)
        high_part = flat.astype(jnp.bfloat16).astype(jnp.float32)
        rest = flat - high_part
        middle_part = rest.astype(jnp.bfloat16).astype(jnp.float32)
        lhs[slot, 0:owned, :] = high_part
        lhs[slot, owned : 2 * owned, :] = middle_part
        lhs[slot, 2 * owned : 3 * owned, :] = rest - middle_part

    weight_load.wait()
    weight_swap.wait()
    result = jnp.dot(
        lhs[0].astype(jnp.bfloat16), weight[0], preferred_element_type=jnp.float32
    ) + jnp.dot(lhs[1].astype(jnp.bfloat16), weight[1], preferred_element_type=jnp.float32)
    out_ref[...] = result[0:owned] + result[owned : 2 * owned] + result[2 * owned : 3 * owned]

    sends(0, 0, k_hbm, finish, True)
    sends(1, 0, v_hbm, finish, True)
    if inner == 2:

        @pl.when((i == 1) & (o < outer - 1))
        def _():
            side_copy().wait_send()

    def settle(d, carry):
        b = me - d * inner
        sends(0, d, kv.at[b, 0], finish, False)
        sends(1, d, kv.at[b, 1], finish, False)
        return carry

    lax.fori_loop(1, o + 1, settle, 0)
    for away, j in pairs:
        part_copy(away, j).wait_send()


def on_device(n, nh, queries, key_states, value_states, out_weight, turn_lengths, block_flags):
    rows = queries.shape[0]
    heads = queries.shape[1] // HD
    groups = key_states.shape[1] // HD
    turns = turn_lengths.shape[0]
    owned = turns // n
    depth, width = out_weight.shape
    cols = width // nh
    inner = 2 if n <= 8 else 8
    outer = n // inner
    wide = heads * rows
    dims = (n, inner, rows, heads, groups, turns, owned)
    lhs_rows = -(-3 * owned // 8) * 8
    dma = pltpu.SemaphoreType.DMA
    any_spec = pl.BlockSpec(memory_space=pl.ANY)
    return pl.pallas_call(
        functools.partial(kernel, dims),
        out_shape=jax.ShapeDtypeStruct((owned, cols), jnp.float32),
        in_specs=[any_spec] * 4
        + [
            pl.BlockSpec(memory_space=pltpu.VMEM),
            pl.BlockSpec(memory_space=pltpu.SMEM),
        ],
        out_specs=pl.BlockSpec(memory_space=pltpu.VMEM),
        scratch_shapes=[
            pltpu.VMEM((n, 2, rows, groups * HD), jnp.bfloat16),
            pltpu.VMEM((rows, heads * HD), jnp.bfloat16),
            pltpu.VMEM((wide, HD), jnp.bfloat16),
            pltpu.VMEM((HD, wide), jnp.bfloat16),
            pltpu.VMEM((nh, depth, cols), jnp.bfloat16),
            pltpu.VMEM((1, wide), jnp.float32),
            pltpu.VMEM((1, wide), jnp.float32),
            pltpu.VMEM((HD, wide), jnp.float32),
            pltpu.VMEM((turns * heads, wide), jnp.bfloat16),
            pltpu.VMEM((turns, heads, HD), jnp.float32),
            pltpu.VMEM((nh, n, owned, heads, HD), jnp.float32),
            pltpu.VMEM((nh, lhs_rows, depth), jnp.float32),
            dma((3,)),
            dma((3,)),
            dma((2, outer)),
            dma((2, outer, inner)),
            dma((2, n)),
            dma,
            dma((nh, n)),
            dma((nh, n)),
        ],
        compiler_params=pltpu.CompilerParams(
            collective_id=0, has_side_effects=True, vmem_limit_bytes=56 << 20
        ),
    )(
        queries,
        key_states,
        value_states,
        out_weight,
        turn_lengths.reshape(1, turns),
        block_flags,
    )


def solution(mesh):
    in_specs = (
        P(("conv", "seq"), "head"),
        P(("conv", "seq"), "head"),
        P(("conv", "seq"), "head"),
        P("head", None),
        P("conv"),
        P(("conv", "seq"), None),
    )
    out_specs = P(("conv", "seq"), "head")
    return jax.shard_map(
        functools.partial(on_device, mesh.shape["seq"], mesh.shape["head"]),
        mesh=mesh,
        in_specs=in_specs,
        out_specs=out_specs,
        check_vma=False,
    )
```

```python
import functools
import math

import jax
import jax.numpy as jnp
from jax import lax
from jax.experimental import pallas as pl
from jax.experimental.pallas import tpu as pltpu
from jax.sharding import PartitionSpec as P

HD = 128
CHUNK = 256
MESH = pl.DeviceIdType.MESH
big_negative = -1e30
log_two_e = 1.4426950408889634


def kernel(
    dims,
    q_hbm,
    k_hbm,
    v_hbm,
    w_hbm,
    len_ref,
    flag_ref,
    out_ref,
    kv,
    q_in,
    q_rows,
    q_turned,
    weight,
    top,
    total,
    acc,
    member,
    part,
    parts,
    lhs,
    local_sem,
    weight_sem,
    line_send,
    row_send,
    recv,
    part_send,
    part_recv,
):
    n, inner, rows, heads, groups, turns, owned, pieces = dims
    outer = n // inner
    repeat = heads // groups
    wide = heads * rows
    factor = log_two_e / math.sqrt(HD)
    me = lax.axis_index("seq")
    head = lax.axis_index("head")
    o, i = lax.div(me, inner), lax.rem(me, inner)

    barrier = pltpu.get_barrier_semaphore()
    for j in range(n):
        peer = lax.rem(me + j, n)
        for core in (1 - head, head) if j else (1 - head,):
            pl.semaphore_signal(
                barrier, inc=1, device_id={"seq": peer, "head": core}, device_id_type=MESH
            )

    cols = weight.shape[2]
    loads = [
        pltpu.make_async_copy(q_hbm, q_in, local_sem.at[0]),
    ]
    short = rows // pieces

    def own_piece(kind):
        return (k_hbm, v_hbm)[kind // pieces].at[pl.ds(kind % pieces * short, short)]

    for kind in range(2 * pieces):
        loads.append(
            pltpu.make_async_copy(own_piece(kind), kv.at[me, kind], local_sem.at[1 + kind])
        )
    for load in loads:
        load.start()
    pl.semaphore_wait(barrier, 2 * n - 1)

    def line_copy(kind, d, source):
        b = me - d * inner
        return pltpu.make_async_remote_copy(
            src_ref=source,
            dst_ref=kv.at[b, kind],
            send_sem=line_send.at[kind, d],
            recv_sem=recv.at[kind, b],
            device_id={"seq": lax.rem(me + inner, n)},
            device_id_type=MESH,
        )

    def row_copy(kind, d, j, source):
        b = me - d * inner
        return pltpu.make_async_remote_copy(
            src_ref=source,
            dst_ref=kv.at[b, kind],
            send_sem=row_send.at[kind, d, j],
            recv_sem=recv.at[kind, b],
            device_id={"seq": o * inner + lax.rem(i + j, inner)},
            device_id_type=MESH,
        )

    def sends(kind, d, source, act, own):
        @pl.when(o < outer - 1)
        def _():
            act(line_copy(kind, d, source))

        for j in range(1, inner):
            if own:

                @pl.when(lax.rem(i + j, inner) > i)
                def _():
                    act(row_copy(kind, d, j, source))

            else:
                act(row_copy(kind, d, j, source))

    def begin(copy):
        copy.start()

    def finish(copy):
        copy.wait_send()

    def arrived(kind, b):
        pltpu.make_async_copy(kv.at[b, kind], kv.at[b, kind], recv.at[kind, b]).wait()

    for kind in range(2 * pieces):
        sends(kind, 0, own_piece(kind), begin, True)
    start = pl.multiple_of(head * cols, cols)
    other = pl.multiple_of((1 - head) * cols, cols)
    weight_load = pltpu.make_async_copy(
        w_hbm.at[:, pl.ds(start, cols)], weight.at[0], weight_sem.at[0]
    )
    weight_swap = pltpu.make_async_remote_copy(
        src_ref=w_hbm.at[:, pl.ds(other, cols)],
        dst_ref=weight.at[1],
        send_sem=weight_sem.at[1],
        recv_sem=weight_sem.at[2],
        device_id={"head": 1 - head},
        device_id_type=MESH,
    )
    weight_load.start()
    weight_swap.start()

    for load in loads:
        load.wait()
    for h in range(heads):
        q_rows[h * rows : (h + 1) * rows, :] = q_in[:, h * HD : (h + 1) * HD]
    q_turned[...] = q_rows[...].T

    def attend(b, diagonal):
        if not diagonal:
            seen = jnp.full((1, CHUNK), flag_ref[0, b], jnp.int32) == 1
        for g in range(groups):
            lanes = slice(g * HD, (g + 1) * HD)
            keys = kv[b, :pieces, :, lanes].reshape(rows, HD)
            values = kv[b, pieces:, :, lanes].reshape(rows, HD).T
            for c in range(g * repeat * rows, (g + 1) * repeat * rows, CHUNK):
                here = slice(c, c + CHUNK)
                logit = jnp.dot(keys, q_turned[:, here], preferred_element_type=jnp.float32)
                if diagonal:
                    column = c + lax.broadcasted_iota(jnp.int32, (1, CHUNK), 1)
                    token = column
                    for h in range(1, heads):
                        token = jnp.where(column >= h * rows, column - h * rows, token)
                    key = lax.broadcasted_iota(jnp.int32, (rows, CHUNK), 0)
                    logit = jnp.where(key <= token, logit, big_negative)
                    new_top = jnp.ceil(jnp.max(logit, axis=0, keepdims=True) * factor)
                    shift = new_top
                else:
                    old_top = top[:, here]
                    block_top = jnp.ceil(jnp.max(logit, axis=0, keepdims=True) * factor)
                    new_top = jnp.maximum(old_top, jnp.where(seen, block_top, big_negative))
                    shift = jnp.where(seen, new_top, -big_negative)
                weights = jnp.exp2(logit * factor - shift)
                added = jnp.sum(weights, axis=0, keepdims=True)
                update = jnp.dot(
                    values, weights.astype(jnp.bfloat16), preferred_element_type=jnp.float32
                )
                top[:, here] = new_top
                if diagonal:
                    total[:, here] = added
                    acc[:, here] = update
                else:
                    rescale = jnp.exp2(old_top - new_top)
                    total[:, here] = total[:, here] * rescale + added
                    acc[:, here] = acc[:, here] * rescale + update

    attend(me, True)

    lengths = len_ref[...].astype(jnp.float32)
    row = lax.broadcasted_iota(jnp.int32, (turns * heads, turns), 0)
    turn_of_row = lax.div(row, heads)
    head_of_row = (row - turn_of_row * heads)[:, :1].astype(jnp.float32)
    turn = lax.broadcasted_iota(jnp.int32, (turns * heads, turns), 1)
    spread = jnp.broadcast_to(lengths, (turns * heads, turns))
    starts = jnp.sum(jnp.where(turn < turn_of_row, spread, 0.0), axis=1, keepdims=True)
    length = jnp.sum(jnp.where(turn == turn_of_row, spread, 0.0), axis=1, keepdims=True)
    base = (me * rows).astype(jnp.float32)
    low = head_of_row * rows + jnp.clip(starts - base, 0.0, rows)
    high = head_of_row * rows + jnp.clip(starts + length - base, 0.0, rows)
    column = lax.broadcasted_iota(jnp.int32, (turns * heads, wide), 1).astype(jnp.float32)
    member[...] = jnp.where((column >= low) & (column < high), 1.0, 0.0).astype(jnp.bfloat16)
    share = 1.0 / length

    def row_blocks(d):
        for j in range(1, inner):
            place = lax.rem(i + j, inner)
            b = (o - d) * inner + place

            @pl.when((place < i) | (d > 0))
            def _():
                for kind in range(2 * pieces):
                    arrived(kind, b)
                attend(b, False)

    def step(d, carry):
        b = me - d * inner
        for kind in range(2 * pieces):
            arrived(kind, b)
            sends(kind, d, kv.at[b, kind], begin, False)
        row_blocks(d - 1)
        attend(b, False)
        return carry

    lax.fori_loop(1, o + 1, step, 0)
    row_blocks(o)

    attended = (acc[...] * (1.0 / total[...])).astype(jnp.bfloat16)
    pooled = lax.dot_general(
        member[...],
        attended,
        (((1,), (1,)), ((), ())),
        preferred_element_type=jnp.float32,
    )
    part[...] = (pooled * share).reshape(turns, heads, HD)

    def part_copy(away, j):
        peer = lax.rem(me + j, n)
        return pltpu.make_async_remote_copy(
            src_ref=part.at[pl.ds(peer * owned, owned)],
            dst_ref=parts.at[head, me],
            send_sem=part_send.at[away, j],
            recv_sem=part_recv.at[head, me],
            device_id={"seq": peer, "head": 1 - head if away else head},
            device_id_type=MESH,
        )

    pairs = [(away, j) for j in range(n) for away in (0, 1) if away or j]
    for away, j in pairs:
        part_copy(away, j).start()

    def gather(away, j):
        peer = lax.rem(me + j, n)
        core = 1 - head if away else head
        here = parts.at[core, peer]
        pltpu.make_async_copy(here, here, part_recv.at[core, peer]).wait()
        return parts[core, peer]

    sums = [part[pl.ds(me * owned, owned)], None]
    for away, j in pairs:
        piece = gather(away, j)
        sums[away] = piece if sums[away] is None else sums[away] + piece

    lhs[...] = jnp.zeros_like(lhs)
    for slot, summed in enumerate(sums):
        flat = jnp.concatenate([summed[:, h, :] for h in range(heads)], axis=1)
        high_part = flat.astype(jnp.bfloat16).astype(jnp.float32)
        rest = flat - high_part
        middle_part = rest.astype(jnp.bfloat16).astype(jnp.float32)
        lhs[slot, 0:owned, :] = high_part
        lhs[slot, owned : 2 * owned, :] = middle_part
        lhs[slot, 2 * owned : 3 * owned, :] = rest - middle_part

    weight_load.wait()
    weight_swap.wait()
    result = jnp.dot(
        lhs[0].astype(jnp.bfloat16), weight[0], preferred_element_type=jnp.float32
    ) + jnp.dot(lhs[1].astype(jnp.bfloat16), weight[1], preferred_element_type=jnp.float32)
    out_ref[...] = result[0:owned] + result[owned : 2 * owned] + result[2 * owned : 3 * owned]

    for kind in range(2 * pieces):
        sends(kind, 0, own_piece(kind), finish, True)
    def settle(d, carry):
        b = me - d * inner
        for kind in range(2 * pieces):
            sends(kind, d, kv.at[b, kind], finish, False)
        return carry

    lax.fori_loop(1, o + 1, settle, 0)
    for away, j in pairs:
        part_copy(away, j).wait_send()


def on_device(n, nh, queries, key_states, value_states, out_weight, turn_lengths, block_flags):
    rows = queries.shape[0]
    heads = queries.shape[1] // HD
    groups = key_states.shape[1] // HD
    turns = turn_lengths.shape[0]
    owned = turns // n
    depth, width = out_weight.shape
    cols = width // nh
    inner = 2 if n <= 8 else 8
    outer = n // inner
    wide = heads * rows
    pieces = 2 if rows % 32 == 0 else 1
    dims = (n, inner, rows, heads, groups, turns, owned, pieces)
    lhs_rows = -(-3 * owned // 8) * 8
    dma = pltpu.SemaphoreType.DMA
    any_spec = pl.BlockSpec(memory_space=pl.ANY)
    return pl.pallas_call(
        functools.partial(kernel, dims),
        out_shape=jax.ShapeDtypeStruct((owned, cols), jnp.float32),
        in_specs=[any_spec] * 4
        + [
            pl.BlockSpec(memory_space=pltpu.VMEM),
            pl.BlockSpec(memory_space=pltpu.SMEM),
        ],
        out_specs=pl.BlockSpec(memory_space=pltpu.VMEM),
        scratch_shapes=[
            pltpu.VMEM((n, 2 * pieces, rows // pieces, groups * HD), jnp.bfloat16),
            pltpu.VMEM((rows, heads * HD), jnp.bfloat16),
            pltpu.VMEM((wide, HD), jnp.bfloat16),
            pltpu.VMEM((HD, wide), jnp.bfloat16),
            pltpu.VMEM((nh, depth, cols), jnp.bfloat16),
            pltpu.VMEM((1, wide), jnp.float32),
            pltpu.VMEM((1, wide), jnp.float32),
            pltpu.VMEM((HD, wide), jnp.float32),
            pltpu.VMEM((turns * heads, wide), jnp.bfloat16),
            pltpu.VMEM((turns, heads, HD), jnp.float32),
            pltpu.VMEM((nh, n, owned, heads, HD), jnp.float32),
            pltpu.VMEM((nh, lhs_rows, depth), jnp.float32),
            dma((1 + 2 * pieces,)),
            dma((3,)),
            dma((2 * pieces, outer)),
            dma((2 * pieces, outer, inner)),
            dma((2 * pieces, n)),
            dma((nh, n)),
            dma((nh, n)),
        ],
        compiler_params=pltpu.CompilerParams(
            collective_id=0, has_side_effects=True, vmem_limit_bytes=56 << 20
        ),
    )(
        queries,
        key_states,
        value_states,
        out_weight,
        turn_lengths.reshape(1, turns),
        block_flags,
    )


def solution(mesh):
    in_specs = (
        P(("conv", "seq"), "head"),
        P(("conv", "seq"), "head"),
        P(("conv", "seq"), "head"),
        P("head", None),
        P("conv"),
        P(("conv", "seq"), None),
    )
    out_specs = P(("conv", "seq"), "head")
    return jax.shard_map(
        functools.partial(on_device, mesh.shape["seq"], mesh.shape["head"]),
        mesh=mesh,
        in_specs=in_specs,
        out_specs=out_specs,
        check_vma=False,
    )
```

```python
import functools
import math

import jax
import jax.numpy as jnp
from jax import lax
from jax.experimental import pallas as pl
from jax.experimental.pallas import tpu as pltpu
from jax.sharding import PartitionSpec as P

HD = 128
CHUNK = 256
MESH = pl.DeviceIdType.MESH
big_negative = -1e30
log_two_e = 1.4426950408889634


def kernel(
    dims,
    q_hbm,
    k_hbm,
    v_hbm,
    w_hbm,
    len_ref,
    flag_ref,
    out_ref,
    kv,
    q_in,
    q_rows,
    q_turned,
    weight,
    top,
    total,
    acc,
    member,
    part,
    parts,
    lhs,
    local_sem,
    weight_sem,
    line_send,
    row_send,
    recv,
    part_send,
    part_recv,
):
    n, inner, rows, heads, groups, turns, owned, pieces = dims
    outer = n // inner
    repeat = heads // groups
    wide = heads * rows
    factor = log_two_e / math.sqrt(HD)
    me = lax.axis_index("seq")
    head = lax.axis_index("head")
    o, i = lax.div(me, inner), lax.rem(me, inner)

    barrier = pltpu.get_barrier_semaphore()
    for j in range(n):
        peer = lax.rem(me + j, n)
        for core in (1 - head, head) if j else (1 - head,):
            pl.semaphore_signal(
                barrier, inc=1, device_id={"seq": peer, "head": core}, device_id_type=MESH
            )

    cols = weight.shape[2]
    loads = [
        pltpu.make_async_copy(q_hbm, q_in, local_sem.at[0]),
    ]
    short = rows // pieces

    def own_piece(kind):
        return (k_hbm, v_hbm)[kind // pieces].at[pl.ds(kind % pieces * short, short)]

    for kind in range(2 * pieces):
        loads.append(
            pltpu.make_async_copy(own_piece(kind), kv.at[me, kind], local_sem.at[1 + kind])
        )
    for load in loads:
        load.start()
    pl.semaphore_wait(barrier, 2 * n - 1)

    def line_copy(kind, d, source):
        b = me - d * inner
        return pltpu.make_async_remote_copy(
            src_ref=source,
            dst_ref=kv.at[b, kind],
            send_sem=line_send.at[kind, d],
            recv_sem=recv.at[kind, b],
            device_id={"seq": lax.rem(me + inner, n)},
            device_id_type=MESH,
        )

    def row_copy(kind, d, j, source):
        b = me - d * inner
        return pltpu.make_async_remote_copy(
            src_ref=source,
            dst_ref=kv.at[b, kind],
            send_sem=row_send.at[kind, d, j],
            recv_sem=recv.at[kind, b],
            device_id={"seq": o * inner + lax.rem(i + j, inner)},
            device_id_type=MESH,
        )

    def sends(kind, d, source, act, own):
        @pl.when(o < outer - 1)
        def _():
            act(line_copy(kind, d, source))

        for j in range(1, inner):
            if own:

                @pl.when(lax.rem(i + j, inner) > i)
                def _():
                    act(row_copy(kind, d, j, source))

            else:
                act(row_copy(kind, d, j, source))

    def begin(copy):
        copy.start()

    def finish(copy):
        copy.wait_send()

    def arrived(kind, b):
        pltpu.make_async_copy(kv.at[b, kind], kv.at[b, kind], recv.at[kind, b]).wait()

    for kind in range(2 * pieces):
        sends(kind, 0, own_piece(kind), begin, True)
    start = pl.multiple_of(head * cols, cols)
    other = pl.multiple_of((1 - head) * cols, cols)
    weight_load = pltpu.make_async_copy(
        w_hbm.at[:, pl.ds(start, cols)], weight.at[0], weight_sem.at[0]
    )
    weight_swap = pltpu.make_async_remote_copy(
        src_ref=w_hbm.at[:, pl.ds(other, cols)],
        dst_ref=weight.at[1],
        send_sem=weight_sem.at[1],
        recv_sem=weight_sem.at[2],
        device_id={"head": 1 - head},
        device_id_type=MESH,
    )
    weight_load.start()
    weight_swap.start()

    for load in loads:
        load.wait()
    for h in range(heads):
        q_rows[h * rows : (h + 1) * rows, :] = q_in[:, h * HD : (h + 1) * HD]
    q_turned[...] = q_rows[...].T

    def attend(b, diagonal):
        if not diagonal:
            seen = jnp.full((1, CHUNK), flag_ref[0, b], jnp.int32) == 1
        for g in range(groups):
            lanes = slice(g * HD, (g + 1) * HD)
            keys = kv[b, :pieces, :, lanes].reshape(rows, HD)
            values = kv[b, pieces:, :, lanes].reshape(rows, HD).T
            for c in range(g * repeat * rows, (g + 1) * repeat * rows, CHUNK):
                here = slice(c, c + CHUNK)
                logit = jnp.dot(keys, q_turned[:, here], preferred_element_type=jnp.float32)
                if diagonal:
                    column = c + lax.broadcasted_iota(jnp.int32, (1, CHUNK), 1)
                    token = column
                    for h in range(1, heads):
                        token = jnp.where(column >= h * rows, column - h * rows, token)
                    key = lax.broadcasted_iota(jnp.int32, (rows, CHUNK), 0)
                    logit = jnp.where(key <= token, logit, big_negative)
                    new_top = jnp.ceil(jnp.max(logit, axis=0, keepdims=True) * factor)
                    shift = new_top
                else:
                    old_top = top[:, here]
                    block_top = jnp.ceil(jnp.max(logit, axis=0, keepdims=True) * factor)
                    new_top = jnp.maximum(old_top, jnp.where(seen, block_top, big_negative))
                    shift = jnp.where(seen, new_top, -big_negative)
                weights = jnp.exp2(logit * factor - shift)
                added = jnp.sum(weights, axis=0, keepdims=True)
                update = jnp.dot(
                    values, weights.astype(jnp.bfloat16), preferred_element_type=jnp.float32
                )
                top[:, here] = new_top
                if diagonal:
                    total[:, here] = added
                    acc[:, here] = update
                else:
                    rescale = jnp.exp2(old_top - new_top)
                    total[:, here] = total[:, here] * rescale + added
                    acc[:, here] = acc[:, here] * rescale + update

    attend(me, True)

    lengths = len_ref[...].astype(jnp.float32)
    row = lax.broadcasted_iota(jnp.int32, (turns * heads, turns), 0)
    turn_of_row = lax.div(row, heads)
    head_of_row = (row - turn_of_row * heads)[:, :1].astype(jnp.float32)
    turn = lax.broadcasted_iota(jnp.int32, (turns * heads, turns), 1)
    spread = jnp.broadcast_to(lengths, (turns * heads, turns))
    starts = jnp.sum(jnp.where(turn < turn_of_row, spread, 0.0), axis=1, keepdims=True)
    length = jnp.sum(jnp.where(turn == turn_of_row, spread, 0.0), axis=1, keepdims=True)
    base = (me * rows).astype(jnp.float32)
    low = head_of_row * rows + jnp.clip(starts - base, 0.0, rows)
    high = head_of_row * rows + jnp.clip(starts + length - base, 0.0, rows)
    column = lax.broadcasted_iota(jnp.int32, (turns * heads, wide), 1).astype(jnp.float32)
    member[...] = jnp.where((column >= low) & (column < high), 1.0, 0.0).astype(jnp.bfloat16)
    share = 1.0 / length

    def row_blocks(d):
        for j in range(1, inner):
            place = lax.rem(i + j, inner)
            b = (o - d) * inner + place

            @pl.when((place < i) | (d > 0))
            def _():
                for kind in range(2 * pieces):
                    arrived(kind, b)
                attend(b, False)

    def step(d, carry):
        b = me - d * inner
        for kind in range(2 * pieces):
            arrived(kind, b)
            sends(kind, d, kv.at[b, kind], begin, False)
        attend(b, False)
        row_blocks(d - 1)
        return carry

    lax.fori_loop(1, o + 1, step, 0)
    row_blocks(o)

    attended = (acc[...] * (1.0 / total[...])).astype(jnp.bfloat16)
    pooled = lax.dot_general(
        member[...],
        attended,
        (((1,), (1,)), ((), ())),
        preferred_element_type=jnp.float32,
    )
    part[...] = (pooled * share).reshape(turns, heads, HD)

    def part_copy(away, j):
        peer = lax.rem(me + j, n)
        return pltpu.make_async_remote_copy(
            src_ref=part.at[pl.ds(peer * owned, owned)],
            dst_ref=parts.at[head, me],
            send_sem=part_send.at[away, j],
            recv_sem=part_recv.at[head, me],
            device_id={"seq": peer, "head": 1 - head if away else head},
            device_id_type=MESH,
        )

    pairs = [(away, j) for j in range(n) for away in (0, 1) if away or j]
    for away, j in pairs:
        part_copy(away, j).start()

    def gather(away, j):
        peer = lax.rem(me + j, n)
        core = 1 - head if away else head
        here = parts.at[core, peer]
        pltpu.make_async_copy(here, here, part_recv.at[core, peer]).wait()
        return parts[core, peer]

    sums = [part[pl.ds(me * owned, owned)], None]
    for away, j in pairs:
        piece = gather(away, j)
        sums[away] = piece if sums[away] is None else sums[away] + piece

    lhs[...] = jnp.zeros_like(lhs)
    for slot, summed in enumerate(sums):
        flat = jnp.concatenate([summed[:, h, :] for h in range(heads)], axis=1)
        high_part = flat.astype(jnp.bfloat16).astype(jnp.float32)
        rest = flat - high_part
        middle_part = rest.astype(jnp.bfloat16).astype(jnp.float32)
        lhs[slot, 0:owned, :] = high_part
        lhs[slot, owned : 2 * owned, :] = middle_part
        lhs[slot, 2 * owned : 3 * owned, :] = rest - middle_part

    weight_load.wait()
    weight_swap.wait()
    result = jnp.dot(
        lhs[0].astype(jnp.bfloat16), weight[0], preferred_element_type=jnp.float32
    ) + jnp.dot(lhs[1].astype(jnp.bfloat16), weight[1], preferred_element_type=jnp.float32)
    out_ref[...] = result[0:owned] + result[owned : 2 * owned] + result[2 * owned : 3 * owned]

    for kind in range(2 * pieces):
        sends(kind, 0, own_piece(kind), finish, True)
    def settle(d, carry):
        b = me - d * inner
        for kind in range(2 * pieces):
            sends(kind, d, kv.at[b, kind], finish, False)
        return carry

    lax.fori_loop(1, o + 1, settle, 0)
    for away, j in pairs:
        part_copy(away, j).wait_send()


def on_device(n, nh, queries, key_states, value_states, out_weight, turn_lengths, block_flags):
    rows = queries.shape[0]
    heads = queries.shape[1] // HD
    groups = key_states.shape[1] // HD
    turns = turn_lengths.shape[0]
    owned = turns // n
    depth, width = out_weight.shape
    cols = width // nh
    inner = 2 if n <= 8 else 8
    outer = n // inner
    wide = heads * rows
    pieces = 2 if rows % 32 == 0 else 1
    dims = (n, inner, rows, heads, groups, turns, owned, pieces)
    lhs_rows = -(-3 * owned // 8) * 8
    dma = pltpu.SemaphoreType.DMA
    any_spec = pl.BlockSpec(memory_space=pl.ANY)
    return pl.pallas_call(
        functools.partial(kernel, dims),
        out_shape=jax.ShapeDtypeStruct((owned, cols), jnp.float32),
        in_specs=[any_spec] * 4
        + [
            pl.BlockSpec(memory_space=pltpu.VMEM),
            pl.BlockSpec(memory_space=pltpu.SMEM),
        ],
        out_specs=pl.BlockSpec(memory_space=pltpu.VMEM),
        scratch_shapes=[
            pltpu.VMEM((n, 2 * pieces, rows // pieces, groups * HD), jnp.bfloat16),
            pltpu.VMEM((rows, heads * HD), jnp.bfloat16),
            pltpu.VMEM((wide, HD), jnp.bfloat16),
            pltpu.VMEM((HD, wide), jnp.bfloat16),
            pltpu.VMEM((nh, depth, cols), jnp.bfloat16),
            pltpu.VMEM((1, wide), jnp.float32),
            pltpu.VMEM((1, wide), jnp.float32),
            pltpu.VMEM((HD, wide), jnp.float32),
            pltpu.VMEM((turns * heads, wide), jnp.bfloat16),
            pltpu.VMEM((turns, heads, HD), jnp.float32),
            pltpu.VMEM((nh, n, owned, heads, HD), jnp.float32),
            pltpu.VMEM((nh, lhs_rows, depth), jnp.float32),
            dma((1 + 2 * pieces,)),
            dma((3,)),
            dma((2 * pieces, outer)),
            dma((2 * pieces, outer, inner)),
            dma((2 * pieces, n)),
            dma((nh, n)),
            dma((nh, n)),
        ],
        compiler_params=pltpu.CompilerParams(
            collective_id=0, has_side_effects=True, vmem_limit_bytes=56 << 20
        ),
    )(
        queries,
        key_states,
        value_states,
        out_weight,
        turn_lengths.reshape(1, turns),
        block_flags,
    )


def solution(mesh):
    in_specs = (
        P(("conv", "seq"), "head"),
        P(("conv", "seq"), "head"),
        P(("conv", "seq"), "head"),
        P("head", None),
        P("conv"),
        P(("conv", "seq"), None),
    )
    out_specs = P(("conv", "seq"), "head")
    return jax.shard_map(
        functools.partial(on_device, mesh.shape["seq"], mesh.shape["head"]),
        mesh=mesh,
        in_specs=in_specs,
        out_specs=out_specs,
        check_vma=False,
    )
```
